32 devices in a mesh: groups: 2 (over x), seq: 16 (over z, y, core).
Axes of the slice: x: 2, y: 2, z: 4, core: 2. Of those that a mesh axis runs over, the one named last changes fastest.
Arguments:
- activations: bfloat16 [4096, 8192], P(('groups', 'seq')), parts along dimension 0, may hold values from -6 to 6
- gate_values: bfloat16 [2, 4096, 8192], P(None, ('groups', 'seq')), parts along dimension 1, may hold values from -6 to 6
- accepted: int32 [4096], P(('groups', 'seq')), parts along dimension 0, may hold values 0 or 1
- seg_starts: int32 [4096], P(('groups', 'seq')), parts along dimension 0, may hold values from 0 to 1984, as said below
- mr_taps: bfloat16 [512, 128], replicated, may hold values from -0.5 to 0.5
- lr_rate: float32 [512, 16], replicated, as said below
- lr_angle: float32 [512, 16], replicated, may hold values from -3.140625 to 3.140625
- lr_residue: float32 [2, 512, 16], replicated, may hold values from -5 to 5
Outputs:
- result: bfloat16 [4096, 8192], P(('groups', 'seq')), parts along dimension 0
The draws below stay inside these ranges and needn't reach their ends.
There are 2 independent parts, one for each index of `groups`. The reference program is written for one: setup_inputs(seed, part) draws one part's arguments, and reference() takes and returns one part's arrays. A program takes and returns all parts, laid end to end along the dimension named above; an argument that names none is the same for every part. Nothing has to cross between parts.
Inputs may be any that keep to these rules, and one draw needn't show every extreme that they name: seg_starts[t] is the first position of the draft segment that holds t: never falling, at most t, equal to t where a segment begins, at most 4 segments. `lr_rate`: every rate is positive.
All inputs are finite; a program needn't handle non-finite values. No bound on the sum of `accepted` on one device may be relied on, other than what follows from the above.
Results may differ from the reference program's by a relative error of at most 0.0061.
Values may be sent and summed in bfloat16 or wider, within the bound.
A program may use at most 192 MiB of HBM per device.

```python
import math
import jax
import jax.numpy as jnp
from jax import lax

D = 8192
FILTERS = 512
MODES = 16
TAPS = 128
TOK_DEV = 128
SEQ = 2048


def draw_seg_starts(key, part):
    last_cut = SEQ - TOK_DEV // 2
    random_cuts = jax.random.randint(key, (2,), 1, last_cut + 1, dtype=jnp.int32)
    cut_points = jnp.concatenate([random_cuts, jnp.full((1,), last_cut, jnp.int32)], axis=0)
    position = jnp.arange(SEQ, dtype=jnp.int32)
    chosen = jnp.where(cut_points[:, None] <= position[None, :], cut_points[:, None], 0)
    return jnp.max(chosen, axis=0).astype(jnp.int32)


def draw_lr_rate(key, part):
    key_pick, key_slow, key_fast = jax.random.split(key, 3)
    slow_share = 0.5
    low_rate = 0.2 / SEQ
    high_rate = 2.0 / SEQ
    fast_low = min(0.5 / TOK_DEV, 1.0 / 64.0)
    fast_high = 1.0 / 25.0
    chooser = jax.random.uniform(key_pick, (FILTERS, MODES), jnp.float32)
    slow_rates = jnp.exp(jax.random.uniform(key_slow, (FILTERS, MODES), jnp.float32, math.log(low_rate), math.log(high_rate)))
    fast_rates = jnp.exp(jax.random.uniform(key_fast, (FILTERS, MODES), jnp.float32, math.log(fast_low), math.log(fast_high)))
    return jnp.where(chooser < slow_share, slow_rates, fast_rates).astype(jnp.float32)


def touch_ends(result, own_key, smallest, largest):
    dims = result.shape
    index_at = [jax.random.randint(jax.random.fold_in(own_key, axis), (), 0, dims[axis]) for axis in range(len(dims))]
    result = result.at[tuple(index_at)].set(smallest)
    longest = dims.index(max(dims))
    index_at[longest] = (index_at[longest] + 1) % dims[longest]
    return result.at[tuple(index_at)].set(largest)


def level_of(rng, dims, shards, least, largest):
    def one(dim, shards_of):
        draws = jax.random.uniform(jax.random.fold_in(jax.random.fold_in(rng, 6), dim), (shards_of,), jnp.float32, least / len(shards), largest / len(shards))
        return jnp.repeat(jnp.exp(draws), dims[dim] // shards_of).reshape((-1,) + (1,) * (len(dims) - dim - 1))

    gain = one(*shards[0])
    for cut in shards[1:]:
        gain = gain * one(*cut)
    return gain


def gaussian(own_key, shape, deviation, bound, cuts=(), held_as=jnp.bfloat16):
    entries = deviation * jax.random.normal(own_key, shape, jnp.float32)
    if cuts:
        entries = entries * level_of(own_key, shape, cuts, -0.22, 0.18)
    return jnp.clip(entries, -bound, bound).astype(held_as)


def setup_inputs(seed: int = 0, part: int = 0) -> dict:
    seeds = jax.random.split(jax.random.key(seed), 9)
    part_splits = jax.random.split(jax.random.fold_in(seeds[8], part), 9)
    activations = gaussian(part_splits[0], (SEQ, D), 1.0, 6.0, ((0, 16),))
    gate_values = gaussian(part_splits[1], (2, SEQ, D), 1.0, 6.0, ((1, 16),))
    accepted = touch_ends((jax.random.randint(part_splits[2], (SEQ,), 0, 4) < 3).astype(jnp.int32), jax.random.fold_in(part_splits[2], 1), 0, 1)
    seg_starts = draw_seg_starts(jax.random.fold_in(jax.random.fold_in(seeds[8], part), 71), part)
    mr_taps = gaussian(seeds[4], (FILTERS, TAPS), TAPS ** -0.5, 0.5)
    lr_rate = draw_lr_rate(jax.random.fold_in(seeds[8], 71), part)
    lr_angle = jnp.clip(jax.random.uniform(seeds[6], (FILTERS, MODES), jnp.float32, -3.140625, 3.140625), -3.140625, 3.140625)
    lr_residue = gaussian(seeds[7], (2, FILTERS, MODES), 1.0, 5.0, (), jnp.float32)
    return {"activations": activations, "gate_values": gate_values, "accepted": accepted, "seg_starts": seg_starts, "mr_taps": mr_taps, "lr_rate": lr_rate, "lr_angle": lr_angle, "lr_residue": lr_residue}


highest = lax.Precision.HIGHEST

def lag_onehot(row_count, col_count, offset, lag_count):
    row_idx = jnp.arange(row_count, dtype=jnp.int32)[:, None, None]
    col_idx = jnp.arange(col_count, dtype=jnp.int32)[None, :, None]
    lag_idx = jnp.arange(lag_count, dtype=jnp.int32)[None, None, :]
    return (row_idx + offset - col_idx == lag_idx).astype(jnp.float32)

def lr_tables(lr_rate, lr_angle, lr_residue, length):
    lag_steps = jnp.arange(length, dtype=jnp.float32)
    rate_col = lr_rate[:, :, None]
    angle_col = lr_angle[:, :, None]
    magnitude = jnp.exp(-rate_col * lag_steps)
    pow_re = magnitude * jnp.cos(angle_col * lag_steps)
    pow_im = magnitude * jnp.sin(angle_col * lag_steps)
    res_scale = 0.25 * jnp.sqrt(lr_rate)
    res_re = (res_scale * lr_residue[0])[:, :, None]
    res_im = (res_scale * lr_residue[1])[:, :, None]
    filter_taps = lax.optimization_barrier(jnp.sum(res_re * pow_re - res_im * pow_im, axis=1)).astype(jnp.bfloat16)
    end_re = pow_re[:, :, ::-1]
    end_im = pow_im[:, :, ::-1]
    lag_next = lag_steps + 1.0
    mag_next = jnp.exp(-rate_col * lag_next)
    one_re = mag_next * jnp.cos(angle_col * lag_next)
    one_im = mag_next * jnp.sin(angle_col * lag_next)
    in_re = res_re * one_re - res_im * one_im
    in_im = res_re * one_im + res_im * one_re
    full_mag = jnp.exp(-lr_rate * length)
    full_re = full_mag * jnp.cos(lr_angle * length)
    full_im = full_mag * jnp.sin(lr_angle * length)
    return (filter_taps, end_re, end_im, in_re, in_im, full_re, full_im)

def lr_local(mid_blocks, row_starts, block_begins, tables, toeplitz):
    length = mid_blocks.shape[1]
    positions = block_begins[:, None] + jnp.arange(length, dtype=jnp.int32)[None, :]
    mid_float = mid_blocks.astype(jnp.float32)
    keep = (positions[:, None, :] >= row_starts[:, :, None]).astype(jnp.float32)
    masked_toep = toeplitz.astype(jnp.float32)[None] * keep[:, None]
    within = jnp.einsum('bgtj,bjgc->btgc', masked_toep, mid_float, precision=highest)
    last_start = row_starts[:, -1]
    keep_rows = (positions >= last_start[:, None]).astype(jnp.float32)
    kept = mid_float * keep_rows[:, :, None, None]
    b_re = jnp.einsum('gmj,bjgc->bgmc', tables[1], kept, precision=highest)
    b_im = jnp.einsum('gmj,bjgc->bgmc', tables[2], kept, precision=highest)
    carry_on = (last_start < block_begins).astype(jnp.float32)[:, None, None]
    a_re = tables[5][None] * carry_on
    a_im = tables[6][None] * carry_on
    inside = (row_starts < block_begins[:, None]).astype(jnp.float32)
    return (within, (a_re, a_im, b_re, b_im), inside)

def incoming(state_re, state_im, in_re, in_im, inside):
    added = jnp.einsum('gmt,bgmc->btgc', in_re, state_re, precision=highest)
    added = added - jnp.einsum('gmt,bgmc->btgc', in_im, state_im, precision=highest)
    return added * inside[:, :, None, None]

def reference(activations, gate_values, accepted, seg_starts, mr_taps, lr_rate, lr_angle, lr_residue):
    tok_rows = TOK_DEV
    rim_rows = TAPS - 1
    channels = D // FILTERS
    win_rows = tok_rows + rim_rows
    masked_input = activations * accepted[:, None].astype(jnp.bfloat16)
    padded = jnp.concatenate([jnp.zeros((rim_rows, D), jnp.bfloat16), masked_input], axis=0)
    onehot = lag_onehot(tok_rows, win_rows, rim_rows, TAPS)
    mr_toeplitz = jnp.einsum('tsk,gk->gts', onehot, mr_taps.astype(jnp.float32), precision=highest).astype(jnp.bfloat16)
    tables = lr_tables(lr_rate, lr_angle, lr_residue, tok_rows)
    lr_toeplitz = jnp.einsum('tjk,gk->gtj', lag_onehot(tok_rows, tok_rows, 0, tok_rows), tables[0].astype(jnp.float32), precision=highest).astype(jnp.bfloat16)

    def advance(carried, block_index):
        block_start = block_index * tok_rows
        window = lax.dynamic_slice_in_dim(padded, block_start, win_rows, 0)
        row_starts = lax.dynamic_slice_in_dim(seg_starts, block_start, tok_rows, 0)
        gate_mr = lax.dynamic_slice_in_dim(gate_values[0], block_start, tok_rows, 0)
        gate_lr = lax.dynamic_slice_in_dim(gate_values[1], block_start, tok_rows, 0)
        col_pos = block_start - rim_rows + jnp.arange(win_rows, dtype=jnp.int32)
        same_segment = (col_pos[None, :] >= row_starts[:, None]).astype(jnp.bfloat16)
        masked_toep = (mr_toeplitz * same_segment[None]).astype(jnp.float32)
        window_float = window.reshape(win_rows, FILTERS, channels).astype(jnp.float32)
        mr_out = jnp.einsum('gts,sgc->tgc', masked_toep, window_float, precision=highest).reshape(tok_rows, D)
        mid_out = (gate_mr.astype(jnp.float32) * mr_out).astype(jnp.bfloat16)
        begins = jnp.reshape(block_start, (1,)).astype(jnp.int32)
        within, summary, inside = lr_local(mid_out.reshape(1, tok_rows, FILTERS, channels), row_starts[None], begins, tables, lr_toeplitz)
        lr_out = within + incoming(carried[0][None], carried[1][None], tables[3], tables[4], inside)
        a_re, a_im, b_re, b_im = summary
        next_re = a_re[0][:, :, None] * carried[0] - a_im[0][:, :, None] * carried[1] + b_re[0]
        next_im = a_re[0][:, :, None] * carried[1] + a_im[0][:, :, None] * carried[0] + b_im[0]
        lr_round = lax.optimization_barrier(lr_out.reshape(tok_rows, D).astype(jnp.bfloat16))
        block_out = (gate_lr.astype(jnp.float32) * lr_round.astype(jnp.float32)).astype(jnp.bfloat16)
        return ((next_re, next_im), block_out)
    initial = (jnp.zeros((FILTERS, MODES, channels), jnp.float32), jnp.zeros((FILTERS, MODES, channels), jnp.float32))
    final_state, blocks = lax.scan(advance, initial, jnp.arange(SEQ // tok_rows, dtype=jnp.int32))
    return blocks.reshape(SEQ, D)
```

```python
import functools
import jax
import jax.numpy as jnp
from jax import lax
from jax.experimental import pallas as pl
from jax.experimental.pallas import tpu as pltpu
from jax.sharding import PartitionSpec as P

f32 = jnp.float32
bf16 = jnp.bfloat16
MESH = pl.DeviceIdType.MESH
LANES = 128


def powers(lam_re, lam_im, exps):
    out_re = jnp.ones(exps.shape, f32)
    out_im = jnp.zeros(exps.shape, f32)
    base_re, base_im = lam_re, lam_im
    for bit in range(7):
        on = ((exps >> bit) & 1) == 1
        new_re = out_re * base_re - out_im * base_im
        new_im = out_re * base_im + out_im * base_re
        out_re = jnp.where(on, new_re, out_re)
        out_im = jnp.where(on, new_im, out_im)
        base_re, base_im = base_re * base_re - base_im * base_im, 2.0 * base_re * base_im
    return out_re, out_im


def outer(a_re, a_im, b_re, b_im, flip):
    res, ims = [], []
    for a in range(8):
        row = 7 - a if flip else a
        pr, pi = a_re[row : row + 1], a_im[row : row + 1]
        res.append(pr * b_re - pi * b_im)
        ims.append(pr * b_im + pi * b_re)
    return jnp.concatenate(res, 0), jnp.concatenate(ims, 0)


def circulant(row):
    wide = jnp.broadcast_to(row, (LANES, LANES))
    return pltpu.roll(wide, 1, 1, stride=1, stride_axis=0).astype(bf16)


def mid_kernel(prev_ref, cur_ref, gate_ref, taps_ref, lam_ref, ma_ref, mb_ref, keep_ref,
               mid_ref, b_ref, near_ref, toep):
    for g in range(8):
        c = circulant(taps_ref[g : g + 1, :])
        toep[g * 128 : (g + 1) * 128, :128] = c * ma_ref[...]
        toep[g * 128 : (g + 1) * 128, 128:] = c * mb_ref[...]
    window = jnp.concatenate([prev_ref[...], cur_ref[...]], axis=0)
    full = jnp.dot(toep[...], window, preferred_element_type=f32)
    group = lax.broadcasted_iota(jnp.int32, (128, LANES), 1) // 16
    mr = full[:128]
    for g in range(1, 8):
        mr = jnp.where(group == g, full[g * 128 : (g + 1) * 128], mr)
    mid = (gate_ref[...].astype(f32) * mr).astype(bf16)
    mid_ref[...] = mid
    lam_re, lam_im = lam_ref[0:1, :], lam_ref[1:2, :]
    res_re, res_im = lam_ref[2:3, :], lam_ref[3:4, :]
    rows8 = lax.broadcasted_iota(jnp.int32, (8, LANES), 0) * 16
    rows16 = 15 - lax.broadcasted_iota(jnp.int32, (16, LANES), 0)
    a_re, a_im = powers(lam_re, lam_im, rows8)
    p_re, p_im = powers(lam_re, lam_im, rows16)
    end_re, end_im = outer(a_re, a_im, p_re, p_im, True)
    kept = mid * keep_ref[...]
    group16 = lax.broadcasted_iota(jnp.int32, (16, LANES), 1) // 16
    parts = []
    for table in (end_re, end_im):
        whole = lax.dot_general(table.astype(bf16), kept, (((0,), (0,)), ((), ())),
                                preferred_element_type=f32)
        got = whole[:16]
        for g in range(1, 8):
            got = jnp.where(group16 == g, whole[g * 16 : (g + 1) * 16], got)
        parts.append(got)
    b_ref[...] = jnp.concatenate(parts, 0).astype(bf16)
    real = res_re * end_re - res_im * end_im
    pick = (lax.broadcasted_iota(jnp.int32, (8, LANES), 1) // 16
            == lax.broadcasted_iota(jnp.int32, (8, LANES), 0)).astype(f32)
    near = lax.dot_general(pick, real, (((1,), (1,)), ((), ())),
                           precision=lax.Precision.HIGHEST, preferred_element_type=f32)
    near_ref[...] = near.astype(bf16).astype(f32)


def out_kernel(mid_ref, near_ref, state_ref, lam_ref, gate_ref, mb_ref, in_ref, out_ref, toep):
    for g in range(8):
        c = circulant(near_ref[g : g + 1, :])
        half = (g % 2) * 128
        row = (g // 2) * 128
        toep[row : row + 128, half : half + 128] = c * mb_ref[...]
    mid = mid_ref[...]
    group = lax.broadcasted_iota(jnp.int32, (128, LANES), 1) // 16
    even = (group % 2 == 0).astype(bf16)
    window = jnp.concatenate([mid * even, mid * (1 - even)], axis=0)
    full = jnp.dot(toep[...], window, preferred_element_type=f32)
    lr = full[:128]
    for g in range(1, 4):
        lr = jnp.where(group // 2 == g, full[g * 128 : (g + 1) * 128], lr)
    lam_re, lam_im = lam_ref[0:1, :], lam_ref[1:2, :]
    res_re, res_im = lam_ref[2:3, :], lam_ref[3:4, :]
    rows8 = lax.broadcasted_iota(jnp.int32, (8, LANES), 0) * 16
    rows16 = 1 + lax.broadcasted_iota(jnp.int32, (16, LANES), 0)
    a_re, a_im = powers(lam_re, lam_im, rows8)
    p_re, p_im = powers(lam_re, lam_im, rows16)
    q_re = res_re * p_re - res_im * p_im
    q_im = res_re * p_im + res_im * p_re
    in_re, in_im = outer(a_re, a_im, q_re, q_im, False)
    inside = in_ref[...]
    table = jnp.concatenate([in_re.astype(bf16) * inside, (-in_im).astype(bf16) * inside], 1)
    group16 = lax.broadcasted_iota(jnp.int32, (16, LANES), 1) // 16
    spread = []
    for ri in range(2):
        part = state_ref[ri * 16 : (ri + 1) * 16, :]
        for g in range(8):
            spread.append(part * (group16 == g).astype(bf16))
    lr = lr + jnp.dot(table, jnp.concatenate(spread, 0), preferred_element_type=f32)
    rounded = lr.astype(bf16).astype(f32)
    out_ref[...] = (gate_ref[...].astype(f32) * rounded).astype(bf16)


def scan_kernel(n, b_ref, flag_ref, a_ref, out_ref, recv, flags, pbuf, land, ss, rs, fs, fr, s2, r2):
    me = lax.axis_index("seq")
    width = recv.shape[2]
    barrier = pltpu.get_barrier_semaphore()
    for k in range(1, n):
        pl.semaphore_signal(barrier, inc=1, device_id={"seq": lax.rem(me + k, n)}, device_id_type=MESH)
    pl.semaphore_wait(barrier, n - 1)

    def lanes(d):
        return pl.ds(pl.multiple_of(d * width, 128), width)

    def copies(k):
        d = lax.rem(me + k, n)
        one = pltpu.make_async_remote_copy(
            src_ref=b_ref.at[:, lanes(d)], dst_ref=recv.at[me], send_sem=ss.at[k],
            recv_sem=rs.at[k], device_id={"seq": d}, device_id_type=MESH)
        two = pltpu.make_async_remote_copy(
            src_ref=flag_ref, dst_ref=flags.at[me], send_sem=fs.at[k],
            recv_sem=fr.at[k], device_id={"seq": d}, device_id_type=MESH)
        return one, two

    def back(k):
        d = lax.rem(me + k, n)
        return pltpu.make_async_remote_copy(
            src_ref=pbuf.at[d], dst_ref=land.at[:, lanes(me)], send_sem=s2.at[k],
            recv_sem=r2.at[k], device_id={"seq": d}, device_id_type=MESH)

    def send(k, _):
        one, two = copies(k)
        one.start()
        two.start()
        return 0

    lax.fori_loop(1, n, send, 0)
    recv[me] = b_ref[:, lanes(me)]
    flags[me] = flag_ref[...]

    def await_(k, _):
        one, two = copies(k)
        one.wait()
        two.wait()
        return 0

    lax.fori_loop(1, n, await_, 0)
    a_re, a_im = a_ref[:16], a_ref[16:]

    def step(i, carry):
        s_re, s_im = carry
        pbuf[i, :16] = s_re.astype(bf16)
        pbuf[i, 16:] = s_im.astype(bf16)
        go = flags[i][0:1, 0:1]
        f_re, f_im = a_re * go, a_im * go
        piece = recv[i].astype(f32)
        return (f_re * s_re - f_im * s_im + piece[:16], f_re * s_im + f_im * s_re + piece[16:])

    zero = jnp.zeros((16, width), f32)
    lax.fori_loop(0, n, step, (zero, zero))

    def send2(k, _):
        back(k).start()
        return 0

    lax.fori_loop(1, n, send2, 0)
    land[:, lanes(me)] = pbuf[me]

    def await2(k, _):
        back(k).wait()
        return 0

    lax.fori_loop(1, n, await2, 0)
    out_ref[...] = land[...]


def shards(activations, gate_values, accepted, seg_starts, mr_taps, lr_rate, lr_angle, lr_residue):
    rows, width = activations.shape
    groups, taps = mr_taps.shape
    modes = lr_rate.shape[1]
    chans = width // groups
    n = lax.axis_size("seq")
    me = lax.axis_index("seq")
    start = me * rows
    pairs = [(i, i + 1) for i in range(n - 1)]
    prev = lax.ppermute(activations, "seq", pairs)
    acc = accepted.astype(f32)
    acc_prev = lax.ppermute(acc, "seq", pairs)

    t = jnp.arange(rows, dtype=jnp.int32)[:, None]
    j = jnp.arange(rows, dtype=jnp.int32)[None, :]
    first = seg_starts[:, None] - start
    ma = ((j > t) & (j - rows >= first)).astype(bf16) * acc_prev[None, :].astype(bf16)
    within = (j <= t) & (j >= first)
    mb_lr = within.astype(bf16)
    mb_mr = mb_lr * acc[None, :].astype(bf16)
    last = seg_starts[-1] - start
    keep = jnp.broadcast_to((t >= last), (rows, LANES)).astype(bf16)
    inside = jnp.broadcast_to((first < 0), (rows, LANES)).astype(bf16)
    flag = jnp.broadcast_to((last < 0).astype(f32), (8, LANES))

    mag = jnp.exp(-lr_rate)
    scale = 0.25 * jnp.sqrt(lr_rate)
    lam = jnp.stack([mag * jnp.cos(lr_angle), mag * jnp.sin(lr_angle),
                     scale * lr_residue[0], scale * lr_residue[1]], 0).reshape(4, groups * modes)
    span = width // n
    own = span // chans
    own_rate = lax.dynamic_slice_in_dim(lr_rate, me * own, own, 0)
    own_angle = lax.dynamic_slice_in_dim(lr_angle, me * own, own, 0)
    own_mag = jnp.exp(-own_rate * rows)
    decay = jnp.concatenate([(own_mag * jnp.cos(own_angle * rows)).T,
                             (own_mag * jnp.sin(own_angle * rows)).T], 0)
    decay = jnp.repeat(decay, chans, axis=1)
    back_taps = mr_taps[:, ::-1].astype(f32)

    tiles = width // LANES
    wide = pl.BlockSpec((rows, LANES), lambda i: (0, i))
    gate = lambda which: pl.BlockSpec((None, rows, LANES), lambda i: (which, 0, i))
    taps_spec = pl.BlockSpec((8, taps), lambda i: (i, 0))
    lam_spec = pl.BlockSpec((4, LANES), lambda i: (0, i))
    mask = pl.BlockSpec((rows, LANES), lambda i: (0, 0))
    state_spec = pl.BlockSpec((2 * modes, LANES), lambda i: (0, i))
    mid, b, near = pl.pallas_call(
        mid_kernel,
        grid=(tiles,),
        in_specs=[wide, wide, gate(0), taps_spec, lam_spec, mask, mask, mask],
        out_specs=[wide, state_spec, taps_spec],
        out_shape=[jax.ShapeDtypeStruct((rows, width), bf16),
                   jax.ShapeDtypeStruct((2 * modes, width), bf16),
                   jax.ShapeDtypeStruct((groups, taps), f32)],
        scratch_shapes=[pltpu.VMEM((8 * rows, 2 * rows), bf16)],
        name="mid",
    )(prev, activations, gate_values, back_taps, lam, ma, mb_mr, keep)

    dma = pltpu.SemaphoreType.DMA((n,))
    vmem = pl.BlockSpec(memory_space=pltpu.VMEM)
    state = pl.pallas_call(
        functools.partial(scan_kernel, n),
        in_specs=[vmem] * 3,
        out_specs=vmem,
        out_shape=jax.ShapeDtypeStruct((2 * modes, width), bf16),
        scratch_shapes=[pltpu.VMEM((n, 2 * modes, span), bf16), pltpu.VMEM((n, 8, LANES), f32),
                        pltpu.VMEM((n, 2 * modes, span), bf16), pltpu.VMEM((2 * modes, width), bf16),
                        dma, dma, dma, dma, dma, dma],
        compiler_params=pltpu.CompilerParams(collective_id=0, has_side_effects=True),
        name="scan",
    )(b, flag, decay)

    return pl.pallas_call(
        out_kernel,
        grid=(tiles,),
        in_specs=[wide, taps_spec, state_spec, lam_spec, gate(1), mask, mask],
        out_specs=wide,
        out_shape=jax.ShapeDtypeStruct((rows, width), bf16),
        scratch_shapes=[pltpu.VMEM((4 * rows, 2 * rows), bf16)],
        name="out",
    )(mid, near, state, lam, gate_values, mb_lr, inside)


def solution(mesh):
    return jax.shard_map(
        shards,
        mesh=mesh,
        in_specs=(P(("groups", "seq"), None), P(None, ("groups", "seq"), None), P(("groups", "seq")),
                  P(("groups", "seq")), P(), P(), P(), P()),
        out_specs=P(("groups", "seq"), None),
        check_vma=False,
    )
```

```python
import functools
import jax
import jax.numpy as jnp
from jax import lax
from jax.experimental import pallas as pl
from jax.experimental.pallas import tpu as pltpu
from jax.sharding import PartitionSpec as P

f32 = jnp.float32
bf16 = jnp.bfloat16
MESH = pl.DeviceIdType.MESH
LANES = 128


def powers(lam_re, lam_im, exps):
    out_re = jnp.ones(exps.shape, f32)
    out_im = jnp.zeros(exps.shape, f32)
    base_re, base_im = lam_re, lam_im
    for bit in range(7):
        on = ((exps >> bit) & 1) == 1
        new_re = out_re * base_re - out_im * base_im
        new_im = out_re * base_im + out_im * base_re
        out_re = jnp.where(on, new_re, out_re)
        out_im = jnp.where(on, new_im, out_im)
        base_re, base_im = base_re * base_re - base_im * base_im, 2.0 * base_re * base_im
    return out_re, out_im


def outer(a_re, a_im, b_re, b_im, flip):
    res, ims = [], []
    for a in range(8):
        row = 7 - a if flip else a
        pr, pi = a_re[row : row + 1], a_im[row : row + 1]
        res.append(pr * b_re - pi * b_im)
        ims.append(pr * b_im + pi * b_re)
    return jnp.concatenate(res, 0), jnp.concatenate(ims, 0)


def circulant(row):
    wide = jnp.broadcast_to(row, (LANES, LANES))
    return pltpu.roll(wide, 1, 1, stride=1, stride_axis=0).astype(bf16)


def mid_tile(prev, cur, gate, taps, lam, masks, toep):
    ma, mb, keep = masks
    for g in range(8):
        c = circulant(taps[g : g + 1, :])
        toep[g * 128 : (g + 1) * 128, :128] = c * ma[...]
        toep[g * 128 : (g + 1) * 128, 128:] = c * mb[...]
    full = jnp.dot(toep[...], jnp.concatenate([prev, cur], axis=0), preferred_element_type=f32)
    group = lax.broadcasted_iota(jnp.int32, (128, LANES), 1) // 16
    mr = full[:128]
    for g in range(1, 8):
        mr = jnp.where(group == g, full[g * 128 : (g + 1) * 128], mr)
    mid = (gate.astype(f32) * mr).astype(bf16)
    lam_re, lam_im, res_re, res_im = lam[0:1], lam[1:2], lam[2:3], lam[3:4]
    rows8 = lax.broadcasted_iota(jnp.int32, (8, LANES), 0) * 16
    rows16 = 15 - lax.broadcasted_iota(jnp.int32, (16, LANES), 0)
    a_re, a_im = powers(lam_re, lam_im, rows8)
    p_re, p_im = powers(lam_re, lam_im, rows16)
    end_re, end_im = outer(a_re, a_im, p_re, p_im, True)
    kept = mid * keep[...]
    group16 = lax.broadcasted_iota(jnp.int32, (16, LANES), 1) // 16
    parts = []
    for table in (end_re, end_im):
        whole = lax.dot_general(table.astype(bf16), kept, (((0,), (0,)), ((), ())),
                                preferred_element_type=f32)
        got = whole[:16]
        for g in range(1, 8):
            got = jnp.where(group16 == g, whole[g * 16 : (g + 1) * 16], got)
        parts.append(got)
    real = res_re * end_re - res_im * end_im
    pick = (lax.broadcasted_iota(jnp.int32, (8, LANES), 1) // 16
            == lax.broadcasted_iota(jnp.int32, (8, LANES), 0)).astype(f32)
    near = lax.dot_general(pick, real, (((1,), (1,)), ((), ())),
                           precision=lax.Precision.HIGHEST, preferred_element_type=f32)
    return mid, jnp.concatenate(parts, 0).astype(bf16), near.astype(bf16).astype(f32)


def near_tile(mid, near, mb, toep):
    for g in range(8):
        c = circulant(near[g : g + 1, :])
        half = (g % 2) * 128
        row = (g // 2) * 128
        toep[row : row + 128, half : half + 128] = c * mb[...]
    group = lax.broadcasted_iota(jnp.int32, (128, LANES), 1) // 16
    even = (group % 2 == 0).astype(bf16)
    window = jnp.concatenate([mid * even, mid * (1 - even)], axis=0)
    full = jnp.dot(toep[:512, :], window, preferred_element_type=f32)
    lr = full[:128]
    for g in range(1, 4):
        lr = jnp.where(group // 2 == g, full[g * 128 : (g + 1) * 128], lr)
    return lr


def far_tile(lr, state, lam, gate, inside):
    lam_re, lam_im, res_re, res_im = lam[0:1], lam[1:2], lam[2:3], lam[3:4]
    rows8 = lax.broadcasted_iota(jnp.int32, (8, LANES), 0) * 16
    rows16 = 1 + lax.broadcasted_iota(jnp.int32, (16, LANES), 0)
    a_re, a_im = powers(lam_re, lam_im, rows8)
    p_re, p_im = powers(lam_re, lam_im, rows16)
    q_re = res_re * p_re - res_im * p_im
    q_im = res_re * p_im + res_im * p_re
    in_re, in_im = outer(a_re, a_im, q_re, q_im, False)
    table = jnp.concatenate([in_re.astype(bf16) * inside[...], (-in_im).astype(bf16) * inside[...]], 1)
    group16 = lax.broadcasted_iota(jnp.int32, (16, LANES), 1) // 16
    spread = []
    for ri in range(2):
        for g in range(8):
            spread.append(state[ri * 16 : (ri + 1) * 16, :] * (group16 == g).astype(bf16))
    lr = lr + jnp.dot(table, jnp.concatenate(spread, 0), preferred_element_type=f32)
    return (gate.astype(f32) * lr.astype(bf16).astype(f32)).astype(bf16)


def kernel(n, unroll, act, gates, taps, lam, ma, mb_mr, mb_lr, keep, inside, flag, decay, out,
           halo, mid, near, lr, bbuf, recv, flags, pbuf, land, toep,
           hs, hr, bs, br, fs, fr, ps, pr):
    me = lax.axis_index("seq")
    span = bbuf.shape[2]
    per = span // LANES
    barrier = pltpu.get_barrier_semaphore()

    def greet(k, _):
        pl.semaphore_signal(barrier, inc=1, device_id={"seq": lax.rem(me + k, n)}, device_id_type=MESH)
        return 0

    lax.fori_loop(1, n, greet, 0)
    pl.semaphore_wait(barrier, n - 1)

    def remote(src, dst, send, recv_sem, to):
        return pltpu.make_async_remote_copy(src_ref=src, dst_ref=dst, send_sem=send, recv_sem=recv_sem,
                                            device_id={"seq": to}, device_id_type=MESH)

    def chunk(q):
        return pl.ds(pl.multiple_of(q * span, 128), span)

    def own(c):
        return lax.rem(me + 1 + c, n)

    def halo_copy(c):
        q = lax.rem(me + 2 + c, n)
        return remote(act.at[:, chunk(q)], halo.at[c], hs.at[c], hr.at[c], lax.rem(me + 1, n))

    def flag_copy(c):
        return remote(flag, flags.at[me], fs.at[c], fr.at[c], own(c))

    def b_copy(c):
        return remote(bbuf.at[c], recv.at[me], bs.at[c], br.at[c], own(c))

    def p_copy(c):
        return remote(pbuf.at[own(c)], land.at[me], ps.at[c], pr.at[c], own(c))

    def looped(lo, hi, fn):
        def run(i, _):
            fn(i)
            return 0
        lax.fori_loop(lo, hi, run, 0)

    looped(0, n, lambda c: halo_copy(c).start())
    looped(0, n - 1, lambda c: flag_copy(c).start())
    flags[me] = flag[...]

    def tiles(c, fn):
        def group(i):
            for u in range(unroll):
                k = i * unroll + u
                tile = own(c) * per + k
                fn(u, pl.ds(pl.multiple_of(tile * LANES, LANES), LANES),
                   pl.ds(pl.multiple_of(tile * 8, 8), 8),
                   pl.ds(pl.multiple_of(k * LANES, LANES), LANES))
        looped(0, per // unroll, group)

    def first(c):
        halo_copy(c).wait_recv()

        def one(u, lanes, rows, local):
            m, b, nr = mid_tile(halo[c, :, local], act[:, lanes], gates[0, :, lanes], taps[rows, :],
                                lam[:, lanes], (ma, mb_mr, keep), toep.at[u])
            mid[:, lanes] = m
            bbuf[c, :, local] = b
            near[rows, :] = nr

        tiles(c, one)

    def first_send(c):
        first(c)
        b_copy(c).start()

    looped(0, n - 1, first_send)
    first(n - 1)
    recv[me] = bbuf[n - 1]

    def second(c):
        def one(u, lanes, rows, local):
            lr[:, lanes] = near_tile(mid[:, lanes], near[rows, :], mb_lr, toep.at[u])
        tiles(c, one)

    early = n // 4
    looped(0, early, second)
    looped(0, n - 1, lambda c: flag_copy(c).wait())
    looped(0, n - 1, lambda c: b_copy(c).wait())
    a_re, a_im = decay[:16], decay[16:]

    def step(i, carry):
        s_re, s_im = carry
        pbuf[i, :16] = s_re.astype(bf16)
        pbuf[i, 16:] = s_im.astype(bf16)
        go = flags[i][0:1, 0:1]
        f_re, f_im = a_re * go, a_im * go
        piece = recv[i].astype(f32)
        return (f_re * s_re - f_im * s_im + piece[:16], f_re * s_im + f_im * s_re + piece[16:])

    zero = jnp.zeros((16, span), f32)
    lax.fori_loop(0, n, step, (zero, zero))
    looped(0, n - 1, lambda c: p_copy(c).start())
    land[me] = pbuf[me]
    looped(early, n, second)
    looped(0, n - 1, lambda c: p_copy(c).wait())
    looped(0, n, lambda c: halo_copy(c).wait_send())

    def third(c):
        def one(u, lanes, rows, local):
            out[:, lanes] = far_tile(lr[:, lanes], land[own(c), :, local], lam[:, lanes], gates[1, :, lanes], inside)
        tiles(c, one)

    looped(0, n, third)


def shards(activations, gate_values, accepted, seg_starts, mr_taps, lr_rate, lr_angle, lr_residue):
    rows, width = activations.shape
    groups, taps = mr_taps.shape
    modes = lr_rate.shape[1]
    chans = width // groups
    n = lax.axis_size("seq")
    me = lax.axis_index("seq")
    start = me * rows
    pairs = [(i, i + 1) for i in range(n - 1)]
    acc = accepted.astype(f32)
    acc_prev = lax.ppermute(acc, "seq", pairs)

    t = jnp.arange(rows, dtype=jnp.int32)[:, None]
    j = jnp.arange(rows, dtype=jnp.int32)[None, :]
    first = seg_starts[:, None] - start
    ma = ((j > t) & (j - rows >= first)).astype(bf16) * acc_prev[None, :].astype(bf16)
    within = (j <= t) & (j >= first)
    mb_lr = within.astype(bf16)
    mb_mr = mb_lr * acc[None, :].astype(bf16)
    last = seg_starts[-1] - start
    keep = jnp.broadcast_to((t >= last), (rows, LANES)).astype(bf16)
    inside = jnp.broadcast_to((first < 0), (rows, LANES)).astype(bf16)
    flag = jnp.broadcast_to((last < 0).astype(f32), (8, LANES))

    mag = jnp.exp(-lr_rate)
    scale = 0.25 * jnp.sqrt(lr_rate)
    lam = jnp.stack([mag * jnp.cos(lr_angle), mag * jnp.sin(lr_angle),
                     scale * lr_residue[0], scale * lr_residue[1]], 0).reshape(4, groups * modes)
    span = width // n
    own = span // chans
    own_rate = lax.dynamic_slice_in_dim(lr_rate, me * own, own, 0)
    own_angle = lax.dynamic_slice_in_dim(lr_angle, me * own, own, 0)
    own_mag = jnp.exp(-own_rate * rows)
    decay = jnp.concatenate([(own_mag * jnp.cos(own_angle * rows)).T,
                             (own_mag * jnp.sin(own_angle * rows)).T], 0)
    decay = jnp.repeat(decay, chans, axis=1)
    back_taps = mr_taps[:, ::-1].astype(f32)

    per = span // LANES
    unroll = 2 if per % 2 == 0 else 1
    dma = pltpu.SemaphoreType.DMA((n,))
    vmem = pl.BlockSpec(memory_space=pltpu.VMEM)
    both = 2 * modes
    return pl.pallas_call(
        functools.partial(kernel, n, unroll),
        in_specs=[vmem] * 11,
        out_specs=vmem,
        out_shape=jax.ShapeDtypeStruct((rows, width), bf16),
        scratch_shapes=[pltpu.VMEM((n, rows, span), bf16), pltpu.VMEM((rows, width), bf16),
                        pltpu.VMEM((groups, taps), f32), pltpu.VMEM((rows, width), f32),
                        pltpu.VMEM((n, both, span), bf16), pltpu.VMEM((n, both, span), bf16),
                        pltpu.VMEM((n, 8, LANES), f32), pltpu.VMEM((n, both, span), bf16),
                        pltpu.VMEM((n, both, span), bf16),
                        pltpu.VMEM((unroll, 8 * rows, 2 * rows), bf16)] + [dma] * 8,
        compiler_params=pltpu.CompilerParams(collective_id=0, has_side_effects=True,
                                             vmem_limit_bytes=56 * 2**20),
        name="hyena",
    )(activations, gate_values, back_taps, lam, ma, mb_mr, mb_lr, keep, inside, flag, decay)


def solution(mesh):
    return jax.shard_map(
        shards,
        mesh=mesh,
        in_specs=(P(("groups", "seq"), None), P(None, ("groups", "seq"), None), P(("groups", "seq")),
                  P(("groups", "seq")), P(), P(), P(), P()),
        out_specs=P(("groups", "seq"), None),
        check_vma=False,
    )
```
